32 devices in a mesh: member: 8 (over z, x), tile: 4 (over y, core).
Axes of the slice: x: 2, y: 2, z: 4, core: 2. Of those that a mesh axis runs over, the one named last changes fastest.
Arguments:
- ensemble: bfloat16 [256, 128, 320], P('member', 'tile'), may hold values from -6 to 6
- departures: bfloat16 [128, 128, 256], P(('tile', 'member')), may hold values from -6 to 6
- innovations: float32 [128, 128], P(('tile', 'member')), may hold values from -12 to 12
- precision: float32 [128, 128], P(('tile', 'member')), may hold values from 0.2 to 5
- obs_count: int32 [128], P(('tile', 'member')), may hold values from 16 to 128
- tile_counts: int32 [4], replicated, may hold values from 0 to 32, as said below
Outputs:
- analysis: bfloat16 [256, 128, 320], P('member', 'tile')
The draws below stay inside these ranges and needn't reach their ends.
Inputs may be any that keep to these rules, and one draw needn't show every extreme that they name: `tile_counts`: each count is a multiple of 8; all counts sum to 64, and for every tile t the counts of tiles 0 to t - 1 sum to t * 8 * 2 plus or minus at most 8.
All inputs are finite; a program needn't handle non-finite values.
Results may differ from the reference program's by a relative error of at most 0.0049.
Values may be sent and summed in bfloat16 or wider, within the bound.
A program may use at most 64 MiB of HBM per device.

```python
import math
import jax
import jax.numpy as jnp
from jax import lax

K = 256
V = 320
P_SIZE = 128
WORK = 2
ITERS = 6
LOC = 4
COLS = 128
N_MEMBER = 8
N_TILE = 4


def draw_tile_counts(key, part):
    reach = WORK // 2
    walk_key, summit_key = jax.random.split(jax.random.fold_in(key, 11))
    offsets = jax.random.randint(walk_key, (N_TILE + 1,), -reach, reach + 1)
    borders = jnp.arange(N_TILE + 1)
    offsets = jnp.where((borders == 0) | (borders == N_TILE), 0, offsets)
    summit = jax.random.randint(summit_key, (), 1, N_TILE - 1)
    offsets = jnp.where(borders == summit, -reach, offsets)
    offsets = jnp.where(borders == summit + 1, reach, offsets)
    per_tile = WORK + offsets[1:] - offsets[:-1]
    return (per_tile * N_MEMBER).astype(jnp.int32)


def plant(drawn, own_key, low, high):
    dims = drawn.shape
    index_at = [jax.random.randint(jax.random.fold_in(own_key, axis), (), 0, dims[axis]) for axis in range(len(dims))]
    drawn = drawn.at[tuple(index_at)].set(low)
    longest = dims.index(max(dims))
    index_at[longest] = (index_at[longest] + 1) % dims[longest]
    return drawn.at[tuple(index_at)].set(high)


def levels(own_key, shape, cuts, least, top_value):
    level, own = 1.0, jax.random.fold_in(own_key, 6)
    for position, shards_of in cuts:
        steps = jnp.exp(jax.random.uniform(jax.random.fold_in(own, position), (shards_of,), jnp.float32, least / len(cuts), top_value / len(cuts)))
        level = level * jnp.repeat(steps, shape[position] // shards_of).reshape([-1 if axis == position else 1 for axis in range(len(shape))])
    return level


def gaussian(rng, shape, width, bound, cuts=(), held_as=jnp.bfloat16):
    factor_of = levels(rng, shape, cuts, -0.22, 0.18) if cuts else 1.0
    drawn = jax.random.normal(rng, shape, jnp.float32) * width * factor_of
    return jnp.minimum(jnp.maximum(drawn, -bound), bound).astype(held_as)


def setup_inputs(seed: int = 0) -> dict:
    streams_of = jax.random.split(jax.random.key(seed), 7)
    return {
        "ensemble": gaussian(streams_of[0], (K, COLS, V), 1.0, 6.0, ((0, 8), (1, 4))),
        "departures": gaussian(streams_of[1], (COLS, P_SIZE, K), 1.0, 6.0, ((0, 32),)),
        "innovations": gaussian(streams_of[2], (COLS, P_SIZE), 2.0, 12.0, ((0, 32),), jnp.float32),
        "precision": jnp.clip(jnp.exp(math.log(5.0) - 3.218876 * jax.random.uniform(streams_of[3], (COLS, P_SIZE), jnp.float32) ** levels(streams_of[3], (COLS, P_SIZE), ((0, 32),), -0.2, 0.2)), 0.2, 5.0),
        "obs_count": plant(jax.random.randint(streams_of[4], (COLS,), P_SIZE // 8, P_SIZE + 1), jax.random.fold_in(streams_of[4], 1), P_SIZE // 8, P_SIZE).astype(jnp.int32),
        "tile_counts": draw_tile_counts(jax.random.fold_in(streams_of[6], 71), 0),
    }


HIGHEST = lax.Precision.HIGHEST

def prepare(departures, innovations, precision, obs_count):
    row_ids = jnp.arange(departures.shape[1], dtype=jnp.int32)
    weight = jnp.where(row_ids[None, :] < obs_count[:, None], jnp.sqrt(precision), jnp.float32(0.0))
    scaled = (departures.astype(jnp.float32) * weight[:, :, None]).astype(jnp.bfloat16)
    signal = (weight * innovations).astype(jnp.bfloat16)
    return (scaled, signal)

def analyse(columns, scaled, signal):
    members = columns.shape[0]
    states = columns.astype(jnp.float32)
    average = lax.optimization_barrier(jnp.mean(states, axis=0))
    spread = (states - average[None]).astype(jnp.bfloat16)
    scaled_f = scaled.astype(jnp.float32)
    gram_matrix = jnp.einsum('npk,npj->nkj', scaled_f, scaled_f, precision=HIGHEST)
    pull_term = jnp.einsum('npk,np->nk', scaled_f, signal.astype(jnp.float32), precision=HIGHEST)
    identity = jnp.eye(members, dtype=jnp.float32)
    system = gram_matrix + (members - 1.0) * identity
    scale_norm = jnp.sqrt(lax.optimization_barrier(jnp.sum(system * system, axis=(1, 2))))
    root_iter = system / scale_norm[:, None, None]
    inverse_iter = jnp.broadcast_to(identity, system.shape)
    for repeat in range(ITERS):
        factor = 1.5 * identity - 0.5 * jnp.einsum('nij,njk->nik', inverse_iter, root_iter, precision=HIGHEST)
        if repeat + 1 < ITERS:
            root_iter = jnp.einsum('nij,njk->nik', root_iter, factor, precision=HIGHEST)
        inverse_iter = jnp.einsum('nij,njk->nik', factor, inverse_iter, precision=HIGHEST)
    halfway = jnp.einsum('njk,nk->nj', inverse_iter, pull_term, precision=HIGHEST)
    shift_w = jnp.einsum('njk,nk->nj', inverse_iter, halfway, precision=HIGHEST) / scale_norm[:, None]
    transform = (jnp.sqrt((members - 1.0) / scale_norm)[:, None, None] * inverse_iter + shift_w[:, :, None]).astype(jnp.bfloat16)
    update = jnp.einsum('njk,jnv->knv', transform.astype(jnp.float32), spread.astype(jnp.float32), precision=HIGHEST)
    return (average[None] + update).astype(jnp.bfloat16)

def reference(ensemble, departures, innovations, precision, obs_count, tile_counts):
    blocks = COLS // LOC
    states = ensemble.reshape(K, blocks, LOC, V).transpose(1, 0, 2, 3)

    def one_block(pieces):
        block_states, block_dep, block_inn, block_prec, block_count = pieces
        scaled, signal = prepare(block_dep, block_inn, block_prec, block_count)
        return analyse(block_states, scaled, signal)
    analysed = lax.map(one_block, (states, departures.reshape(blocks, LOC, P_SIZE, K), innovations.reshape(blocks, LOC, P_SIZE), precision.reshape(blocks, LOC, P_SIZE), obs_count.reshape(blocks, LOC)))
    analysed = analysed.transpose(1, 0, 2, 3).reshape(K, COLS, V)
    column_ids = jnp.arange(COLS, dtype=jnp.int32)
    tile_of = (column_ids // (N_MEMBER * LOC)).astype(jnp.int32)
    is_live = N_MEMBER * (column_ids % LOC) < jnp.take(tile_counts, tile_of)
    return jnp.where(is_live[None, :, None], analysed, ensemble)
```

```python
import functools

import jax
import jax.numpy as jnp
from jax import lax
from jax.experimental import pallas as pl
from jax.experimental.pallas import tpu as pltpu
from jax.sharding import PartitionSpec as P

WORK = 2
ITERS = 6
LANES = 128
PASSES = (1, 1, 1, 3, 3)
MESH = pl.DeviceIdType.MESH
F32 = jnp.float32
BF16 = jnp.bfloat16


def dot(a, b, ca=1, cb=0):
    return lax.dot_general(a, b, (((ca,), (cb,)), ((), ())), preferred_element_type=F32)


def split(x):
    high = x.astype(BF16)
    return high, (x - high.astype(F32)).astype(BF16)


def mm(a, b, passes):
    if passes == 1:
        return dot(a.astype(BF16), b.astype(BF16))
    ah, al = split(a)
    bh, bl = split(b)
    return dot(ah, bh) + (dot(ah, bl) + dot(al, bh))


def mm_exact(a, b):
    ah, al = split(a)
    return dot(ah, b) + dot(al, b)


def log2(n):
    return n.bit_length() - 1


class Packing:
    def __init__(self, rows, length):
        self.rows, self.length = rows, length
        self.chunk = min(16, rows)
        self.parts = rows // self.chunk
        self.full, self.rest = divmod(length, LANES)
        self.per = LANES // self.rest if self.rest else 1
        self.tails = -(-self.parts // self.per) if self.rest else 0
        self.depth = self.full * rows + self.tails * self.chunk

    def places(self, part):
        found = [
            (pl.ds(f * self.rows + part * self.chunk, self.chunk), slice(0, LANES), slice(f * LANES, (f + 1) * LANES))
            for f in range(self.full)
        ]
        if self.rest:
            down, across = divmod(part, self.per)
            found.append((
                pl.ds(self.full * self.rows + down * self.chunk, self.chunk),
                slice(across * self.rest, (across + 1) * self.rest),
                slice(self.full * LANES, self.length),
            ))
        return found

    def put(self, ref, which, part, piece):
        if part == 0 and self.rest and self.parts % self.per:
            tail = pl.ds(self.full * self.rows, self.tails * self.chunk)
            ref[which, :, tail, :] = jnp.zeros((ref.shape[1], self.tails * self.chunk, LANES), BF16)
        for down, across, of in self.places(part):
            ref[which, :, down, across] = piece[:, :, of].astype(BF16)

    def take(self, ref, which, part):
        return jnp.concatenate(
            [ref[which, :, down, across].astype(F32) for down, across, _ in self.places(part)], axis=2
        )


def kernel(
    tiles, groups, counts_ref, obs_ref, ens_hbm, dep_hbm, inn_hbm, prec_hbm, out_ref,
    ens_ref, dep_ref, inn_ref, prec_ref, load_sem,
    work, mrg_send, mrg_recv, obs_send, obs_recv, cols, ret, home, back,
    mrg_ssem, mrg_rsem, obs_ssem, obs_rsem, in_ssem, in_rsem, out_ssem, out_rsem, fwd_ssem, fwd_rsem,
):
    me = lax.axis_index("member")
    tile = lax.axis_index("tile")
    loads = [
        pltpu.make_async_copy(source, kept, load_sem.at[i])
        for i, (source, kept) in enumerate(
            ((inn_hbm, inn_ref), (prec_hbm, prec_ref), (dep_hbm, dep_ref), (ens_hbm, ens_ref))
        )
    ]
    for load in loads:
        load.start()
    rows, width, length = ens_ref.shape
    capacity, obs_rows, members = dep_ref.shape
    packing = Packing(rows, length)
    both = range(WORK)

    core = lax.rem(tile, 2)
    first = core == 0
    beside = (tile + 1 - 2 * core, tile - 1 + 2 * core)
    has_next = jnp.logical_and(beside[1] >= 0, beside[1] < tiles)
    there = (tile >= 0, has_next)

    barrier = pltpu.get_barrier_semaphore()
    for step in range(1, groups):
        pl.semaphore_signal(barrier, inc=1, device_id=(me ^ step, tile), device_id_type=MESH)
    pl.semaphore_signal(barrier, inc=1, device_id=(me, beside[0]), device_id_type=MESH)

    @pl.when(has_next)
    def _():
        pl.semaphore_signal(barrier, inc=1, device_id=(me, beside[1]), device_id_type=MESH)

    before = 0
    here = 0
    for other in range(tiles):
        count = counts_ref[other]
        before = before + jnp.where(other < tile, count, 0)
        here = here + jnp.where(other == tile, count, 0)
    before = before // groups
    here = here // groups
    lead = before - tile * WORK
    trail = before + here - (tile + 1) * WORK
    top = capacity - 1
    slots = (1 - core, core)
    own = [jnp.clip(slots[i] - lead, 0, top) for i in both]
    send_right = jnp.clip(WORK - lead, 0, top)
    sent = (jnp.where(first, send_right, 0), jnp.where(first, 0, send_right))
    takes = (
        jnp.where(first, trail < 0, lead > 0),
        jnp.where(first, lead > 0, trail < 0),
    )

    eye_obs = lax.broadcasted_iota(jnp.int32, (obs_rows, obs_rows), 0) == lax.broadcasted_iota(
        jnp.int32, (obs_rows, obs_rows), 1
    )
    row_ids = lax.broadcasted_iota(jnp.int32, (1, obs_rows), 1)

    def observe(index):
        weight = jnp.where(row_ids < obs_ref[index], jnp.sqrt(prec_ref[pl.ds(index, 1), :]), 0.0)
        signal = weight * inn_ref[pl.ds(index, 1), :]
        weight_col = jnp.sum(jnp.where(eye_obs, weight, 0.0), axis=1, keepdims=True)
        scaled = dep_ref[index].astype(F32) * weight_col
        return scaled, jnp.broadcast_to(signal, (16, obs_rows))

    for load in loads[:3]:
        load.wait()
    for i in both:
        scaled, signal = observe(sent[i])
        obs_send[i, :obs_rows, :] = scaled.astype(BF16)
        obs_send[i, obs_rows:, :] = jnp.zeros((16, members), BF16)
        obs_send[i, obs_rows:, :obs_rows] = signal.astype(BF16)

    chunk, parts = packing.chunk, packing.parts
    lc, lg, lw, lcap = log2(chunk), log2(groups), log2(width), log2(capacity)
    block = groups * chunk
    out_row = lax.broadcasted_iota(jnp.int32, (2 * WORK * block, 1), 0)
    slot = out_row >> (lc + lg)
    column = jnp.where(
        slot == 0, own[0], jnp.where(slot == 1, own[1], jnp.where(slot == 2, sent[0], sent[1]))
    )
    wanted = (
        ((out_row & (chunk - 1)) << lw) + (((out_row >> lc) & (groups - 1)) << lcap) + column
    )
    in_row = lax.broadcasted_iota(jnp.int32, (2 * WORK * block, chunk * width), 1)
    gather = jnp.where(in_row == wanted, 1.0, 0.0).astype(BF16)
    loads[3].wait()
    for part in range(parts):
        states = ens_ref[pl.ds(part * chunk, chunk)].reshape(chunk * width, length)
        picked = dot(gather, states)
        for s in range(2 * WORK):
            piece = picked[s * block:(s + 1) * block].reshape(groups, chunk, length)
            packing.put(work if s < WORK else mrg_send, s % WORK, part, piece)

    @pl.when(jnp.logical_not(has_next))
    def _():
        mrg_recv[1] = jnp.zeros(mrg_recv.shape[1:], BF16)
        obs_recv[1] = jnp.zeros(obs_recv.shape[1:], BF16)
        back[1] = jnp.zeros(back.shape[1:], BF16)

    pl.semaphore_wait(barrier, groups + jnp.where(has_next, 1, 0))

    def remote(src, dst, ssem, rsem, device):
        return pltpu.make_async_remote_copy(
            src_ref=src, dst_ref=dst, send_sem=ssem, recv_sem=rsem,
            device_id=device, device_id_type=MESH,
        )

    def obs_copy(i):
        return remote(obs_send.at[i], obs_recv.at[i], obs_ssem.at[i], obs_rsem.at[i], (me, beside[i]))

    def mrg_copy(i):
        return remote(mrg_send.at[i], mrg_recv.at[i], mrg_ssem.at[i], mrg_rsem.at[i], (me, beside[i]))

    def in_copy(i, peer, source):
        return remote(work.at[i, peer], cols.at[i, source], in_ssem.at[i], in_rsem.at[i], (peer, tile))

    def in_all(i):
        span = pl.ds(0, groups - 1)
        return remote(work.at[i, span], cols.at[i, span], in_ssem.at[i], in_rsem.at[i], (me ^ 1, tile))

    half = groups // 2

    def out_copy(i, step):
        return remote(
            ret.at[i, me ^ step], home.at[i, step], out_ssem.at[i], out_rsem.at[i, step // half], (me ^ step, tile)
        )

    def out_part(i, part):
        span = pl.ds(0, half - 1 + part)
        return remote(ret.at[i, span], home.at[i, span], out_ssem.at[i], out_rsem.at[i, part], (me ^ 1, tile))

    def out_all(i):
        span = pl.ds(0, groups - 1)
        return remote(ret.at[i, span], home.at[i, span], out_ssem.at[i], out_rsem.at[i, 0], (me ^ 1, tile))

    def fwd_copy(i, part):
        span = pl.ds(part * half, half)
        return remote(
            home.at[i, span], back.at[i, span], fwd_ssem.at[i, part], fwd_rsem.at[i, part], (me, beside[i])
        )

    order = [*range(1, groups)]

    for copy in (mrg_copy, obs_copy):
        for i in (1, 0):

            @pl.when(there[i])
            def _(i=i, copy=copy):
                copy(i).start()

    def spread_out(i):
        @pl.when(there[i])
        def _():
            mrg_copy(i).wait_recv()

        for g in range(groups):
            work[i, g] = jnp.where(takes[i], mrg_recv[i, g].astype(F32), work[i, g].astype(F32)).astype(BF16)

        @pl.when(me >= 0)
        def _():
            for step in order:
                in_copy(i, me ^ step, me).start()
            cols[i, me] = work[i, me]

    base = members - 1.0
    eye = jnp.where(eye_obs, 1.0, 0.0)
    eye_all = lax.broadcasted_iota(jnp.int32, (members, members), 0) == lax.broadcasted_iota(
        jnp.int32, (members, members), 1
    )

    def observations(i):
        ours = observe(own[i])

        @pl.when(there[i])
        def _():
            obs_copy(i).wait_recv()

        took = jnp.where(takes[i], obs_recv[i, :obs_rows, :].astype(F32), ours[0])
        scaled = took.astype(BF16)
        took = jnp.where(takes[i], obs_recv[i, obs_rows:, :obs_rows].astype(F32), ours[1])
        return scaled, took.astype(BF16)

    def transforms(found):
        scaled, signal = zip(*[observations(i) for i in both])
        n = both
        gram = [dot(scaled[w], scaled[w], 1, 1) for w in n]
        norm, x, xc, pc, q, p = [], [], [], [], [], []
        for w in n:
            total = jnp.sum(
                gram[w] * gram[w] + (2.0 * base) * jnp.where(eye_obs, gram[w], 0.0), keepdims=True
            )
            norm.append(jnp.sqrt(total + base * base * members))
            x.append(gram[w] / norm[w])
            xc.append(base / norm[w])
            pc.append(1.5 - 0.5 * xc[w])
            q.append(-0.5 * eye)
            p.append(pc[w] * eye - 0.5 * x[w])
        for repeat in range(ITERS - 1):
            n_pass = PASSES[repeat]
            square = [mm(p[w], p[w], n_pass) for w in n]
            mixed = [
                mm(
                    jnp.concatenate(
                        [square[w], square[w] + pc[w] * p[w] + (pc[w] * pc[w]) * eye], axis=1
                    ),
                    jnp.concatenate([p[w], xc[w] * q[w]], axis=0),
                    n_pass,
                )
                for w in n
            ]
            for w in n:
                q[w] = 1.5 * q[w] - 0.5 * mixed[w]
                pc[w] = pc[w] * (1.5 - 0.5 * xc[w] * pc[w] * pc[w])
            if repeat + 2 < ITERS:
                p = [pc[w] * eye + mm(x[w], q[w], n_pass) for w in n]
            yield

        y = [signal[w].astype(F32) for w in n]
        for _ in range(2):
            y = [pc[w] * y[w] + mm(mm(y[w], q[w], 3), x[w], 3) for w in n]
        shift = [mm_exact(y[w], scaled[w])[:1] / norm[w] for w in n]
        for w in n:
            half = mm_exact(q[w] / norm[w], scaled[w])
            hh, hl = split(half)
            inverse = dot(scaled[w], hh, 0, 0) + dot(scaled[w], hl, 0, 0)
            inverse = inverse + jnp.where(eye_all, pc[w], 0.0)
            found.append((jnp.sqrt(base / norm[w]) * inverse + shift[w]).astype(BF16))
        yield

    def analyse(i, transform):
        in_all(i).wait_recv()
        states = jnp.concatenate([packing.take(cols, i, part) for part in range(parts)], axis=1)
        states = states.reshape(members, length)
        average = jnp.sum(states, axis=0, keepdims=True) * (1.0 / members)
        spread = (states - average).astype(BF16)
        result = (average + dot(transform, spread)).reshape(groups, rows, length)
        for part in range(parts):
            packing.put(ret, i, part, result[:, part * chunk:(part + 1) * chunk])

        @pl.when(me >= 0)
        def _():
            for step in order:
                out_copy(i, step).start()
            home[i, 0] = ret[i, me]

    spread_out(1)
    spread_out(0)
    transform = []
    for _ in transforms(transform):
        pass
    analyse(1, transform[1])
    analyse(0, transform[0])
    for i in both:

        @pl.when(there[i])
        def _(i=i):
            obs_copy(i).wait_send()
            mrg_copy(i).wait_send()

        in_all(i).wait_send()

    back_row = lax.broadcasted_iota(jnp.int32, (chunk * width, 1), 0)
    position = back_row & (capacity - 1)
    live = position < here
    to_left = position < jnp.maximum(-lead, 0)
    to_right = position >= WORK - lead
    line = ((((back_row >> lcap) & (groups - 1)) ^ me) << lc) + (back_row >> lw)
    home_row = lax.broadcasted_iota(jnp.int32, (chunk * width, 2 * block), 1)
    is_first = jnp.full((chunk * width, 1), core, jnp.int32) == 0

    def forward(i):
        for part in range(2):
            out_part(i, part).wait_recv()

            @pl.when(there[i])
            def _(part=part):
                fwd_copy(i, part).start()

    def place(i):
        left_side = is_first if i == 1 else jnp.logical_not(is_first)
        over = jnp.logical_or(
            jnp.logical_and(left_side, to_left),
            jnp.logical_and(jnp.logical_not(left_side), to_right),
        )
        kept_here = jnp.logical_not(jnp.logical_or(to_left, to_right))
        ours = jnp.logical_and(kept_here, position + lead == slots[i])
        mine = jnp.logical_and(live, jnp.logical_or(ours, over))
        target = jnp.where(mine, line + jnp.where(over, block, 0), -1)
        scatter = jnp.where(home_row == target, 1.0, 0.0).astype(BF16)

        @pl.when(there[i])
        def _():
            for part in range(2):
                fwd_copy(i, part).wait_recv()

        for part in range(parts):
            span = pl.ds(part * chunk, chunk)
            found = jnp.concatenate(
                [packing.take(ref, i, part).reshape(block, length).astype(BF16) for ref in (home, back)], axis=0
            )
            placed = dot(scatter, found)
            kept = (ens_ref if i else out_ref)[span].reshape(chunk * width, length).astype(F32)
            placed = jnp.where(mine, placed, kept)
            out_ref[span] = placed.astype(BF16).reshape(chunk, width, length)

    forward(1)
    forward(0)
    place(1)
    place(0)
    for i in both:
        out_all(i).wait_send()

        @pl.when(there[i])
        def _(i=i):
            for part in range(2):
                fwd_copy(i, part).wait_send()


def on_device(ensemble, departures, innovations, precision, obs_count, tile_counts):
    groups = lax.axis_size("member")
    tiles = lax.axis_size("tile")
    rows, width, length = ensemble.shape
    capacity, obs_rows, members = departures.shape
    vmem = pl.BlockSpec(memory_space=pltpu.VMEM)
    smem = pl.BlockSpec(memory_space=pltpu.SMEM)
    hbm = pl.BlockSpec(memory_space=pl.ANY)
    dma = pltpu.SemaphoreType.DMA
    blocks = pltpu.VMEM((WORK, groups, Packing(rows, length).depth, LANES), BF16)
    seen = pltpu.VMEM((WORK, obs_rows + 16, members), BF16)
    return pl.pallas_call(
        functools.partial(kernel, tiles, groups),
        out_shape=pltpu.VMEM(ensemble.shape, BF16),
        in_specs=[smem, smem, hbm, hbm, hbm, hbm],
        out_specs=vmem,
        scratch_shapes=[
            pltpu.VMEM(ensemble.shape, BF16),
            pltpu.VMEM(departures.shape, BF16),
            pltpu.VMEM(innovations.shape, F32),
            pltpu.VMEM(precision.shape, F32),
            dma((4,)),
            blocks, blocks, blocks, seen, seen, blocks, blocks, blocks, blocks,
            dma((WORK,)), dma((WORK,)), dma((WORK,)), dma((WORK,)),
            dma((WORK,)), dma((WORK,)), dma((WORK,)), dma((WORK, 2)), dma((WORK, 2)), dma((WORK, 2)),
        ],
        compiler_params=pltpu.CompilerParams(
            collective_id=0, has_side_effects=True, vmem_limit_bytes=56 * 1024 * 1024
        ),
    )(tile_counts, obs_count, ensemble, departures, innovations, precision)


def solution(mesh):
    placed = (
        P("member", "tile", None),
        P(("tile", "member"), None, None),
        P(("tile", "member"), None),
        P(("tile", "member"), None),
        P(("tile", "member")),
        P(),
    )
    return jax.shard_map(
        on_device, mesh=mesh, in_specs=placed, out_specs=P("member", "tile", None), check_vma=False
    )
```

```python
import functools

import jax
import jax.numpy as jnp
from jax import lax
from jax.experimental import pallas as pl
from jax.experimental.pallas import tpu as pltpu
from jax.sharding import PartitionSpec as P

WORK = 2
ITERS = 6
LANES = 128
PASSES = (1, 1, 1, 3, 3)
MESH = pl.DeviceIdType.MESH
F32 = jnp.float32
BF16 = jnp.bfloat16


def dot(a, b, ca=1, cb=0):
    return lax.dot_general(a, b, (((ca,), (cb,)), ((), ())), preferred_element_type=F32)


def split(x):
    high = x.astype(BF16)
    return high, (x - high.astype(F32)).astype(BF16)


def mm(a, b, passes):
    if passes == 1:
        return dot(a.astype(BF16), b.astype(BF16))
    ah, al = split(a)
    bh, bl = split(b)
    return dot(ah, bh) + (dot(ah, bl) + dot(al, bh))


def mm_exact(a, b):
    ah, al = split(a)
    return dot(ah, b) + dot(al, b)


def log2(n):
    return n.bit_length() - 1


class Packing:
    def __init__(self, rows, length):
        self.rows, self.length = rows, length
        self.chunk = min(16, rows)
        self.parts = rows // self.chunk
        self.full, self.rest = divmod(length, LANES)
        self.per = LANES // self.rest if self.rest else 1
        self.tails = -(-self.parts // self.per) if self.rest else 0
        self.depth = self.full * rows + self.tails * self.chunk

    def places(self, part):
        found = [
            (pl.ds(f * self.rows + part * self.chunk, self.chunk), slice(0, LANES), slice(f * LANES, (f + 1) * LANES))
            for f in range(self.full)
        ]
        if self.rest:
            down, across = divmod(part, self.per)
            found.append((
                pl.ds(self.full * self.rows + down * self.chunk, self.chunk),
                slice(across * self.rest, (across + 1) * self.rest),
                slice(self.full * LANES, self.length),
            ))
        return found

    def put(self, ref, which, part, piece):
        if part == 0 and self.rest and self.parts % self.per:
            tail = pl.ds(self.full * self.rows, self.tails * self.chunk)
            ref[which, :, tail, :] = jnp.zeros((ref.shape[1], self.tails * self.chunk, LANES), BF16)
        for down, across, of in self.places(part):
            ref[which, :, down, across] = piece[:, :, of].astype(BF16)

    def take(self, ref, which, part):
        return jnp.concatenate(
            [ref[which, :, down, across].astype(F32) for down, across, _ in self.places(part)], axis=2
        )


def kernel(
    tiles, groups, counts_ref, obs_ref, ens_hbm, dep_hbm, inn_hbm, prec_hbm, out_ref,
    ens_ref, dep_ref, inn_ref, prec_ref, load_sem,
    work, mrg_send, mrg_recv, obs_send, obs_recv, cols, ret, home, back,
    mrg_ssem, mrg_rsem, obs_ssem, obs_rsem, in_ssem, in_rsem, out_ssem, out_rsem, fwd_ssem, fwd_rsem,
):
    me = lax.axis_index("member")
    tile = lax.axis_index("tile")
    rows, width, length = ens_ref.shape
    capacity, obs_rows, members = dep_ref.shape
    packing = Packing(rows, length)
    both = range(WORK)

    core = lax.rem(tile, 2)
    first = core == 0
    beside = (tile + 1 - 2 * core, tile - 1 + 2 * core)
    has_next = jnp.logical_and(beside[1] >= 0, beside[1] < tiles)
    there = (tile >= 0, has_next)

    barrier = pltpu.get_barrier_semaphore()
    for step in range(groups - 1, 0, -1):
        pl.semaphore_signal(barrier, inc=1, device_id=(me ^ step, tile), device_id_type=MESH)
    pl.semaphore_signal(barrier, inc=1, device_id=(me, beside[0]), device_id_type=MESH)

    @pl.when(has_next)
    def _():
        pl.semaphore_signal(barrier, inc=1, device_id=(me, beside[1]), device_id_type=MESH)

    loads = [
        pltpu.make_async_copy(source, kept, load_sem.at[i])
        for i, (source, kept) in enumerate(
            ((inn_hbm, inn_ref), (prec_hbm, prec_ref), (dep_hbm, dep_ref), (ens_hbm, ens_ref))
        )
    ]
    for load in loads:
        load.start()
    before = 0
    here = 0
    for other in range(tiles):
        count = counts_ref[other]
        before = before + jnp.where(other < tile, count, 0)
        here = here + jnp.where(other == tile, count, 0)
    before = before // groups
    here = here // groups
    lead = before - tile * WORK
    trail = before + here - (tile + 1) * WORK
    top = capacity - 1
    slots = (1 - core, core)
    own = [jnp.clip(slots[i] - lead, 0, top) for i in both]
    send_right = jnp.clip(WORK - lead, 0, top)
    sent = (jnp.where(first, send_right, 0), jnp.where(first, 0, send_right))
    takes = (
        jnp.where(first, trail < 0, lead > 0),
        jnp.where(first, lead > 0, trail < 0),
    )

    eye_obs = lax.broadcasted_iota(jnp.int32, (obs_rows, obs_rows), 0) == lax.broadcasted_iota(
        jnp.int32, (obs_rows, obs_rows), 1
    )
    row_ids = lax.broadcasted_iota(jnp.int32, (1, obs_rows), 1)

    def observe(index):
        weight = jnp.where(row_ids < obs_ref[index], jnp.sqrt(prec_ref[pl.ds(index, 1), :]), 0.0)
        signal = weight * inn_ref[pl.ds(index, 1), :]
        weight_col = jnp.sum(jnp.where(eye_obs, weight, 0.0), axis=1, keepdims=True)
        scaled = dep_ref[index].astype(F32) * weight_col
        return scaled, jnp.broadcast_to(signal, (16, obs_rows))

    for load in loads[:3]:
        load.wait()
    for i in both:
        scaled, signal = observe(sent[i])
        obs_send[i, :obs_rows, :] = scaled.astype(BF16)
        obs_send[i, obs_rows:, :] = jnp.zeros((16, members), BF16)
        obs_send[i, obs_rows:, :obs_rows] = signal.astype(BF16)

    chunk, parts = packing.chunk, packing.parts
    lc, lg, lw, lcap = log2(chunk), log2(groups), log2(width), log2(capacity)
    block = groups * chunk
    out_row = lax.broadcasted_iota(jnp.int32, (2 * WORK * block, 1), 0)
    slot = out_row >> (lc + lg)
    column = jnp.where(
        slot == 0, own[0], jnp.where(slot == 1, own[1], jnp.where(slot == 2, sent[0], sent[1]))
    )
    wanted = (
        ((out_row & (chunk - 1)) << lw) + (((out_row >> lc) & (groups - 1)) << lcap) + column
    )
    in_row = lax.broadcasted_iota(jnp.int32, (2 * WORK * block, chunk * width), 1)
    gather = jnp.where(in_row == wanted, 1.0, 0.0).astype(BF16)
    loads[3].wait()
    for part in range(parts):
        states = ens_ref[pl.ds(part * chunk, chunk)].reshape(chunk * width, length)
        picked = dot(gather, states)
        for s in range(2 * WORK):
            piece = picked[s * block:(s + 1) * block].reshape(groups, chunk, length)
            packing.put(work if s < WORK else mrg_send, s % WORK, part, piece)

    @pl.when(jnp.logical_not(has_next))
    def _():
        mrg_recv[1] = jnp.zeros(mrg_recv.shape[1:], BF16)
        obs_recv[1] = jnp.zeros(obs_recv.shape[1:], BF16)
        back[1] = jnp.zeros(back.shape[1:], BF16)

    pl.semaphore_wait(barrier, groups + jnp.where(has_next, 1, 0))

    def remote(src, dst, ssem, rsem, device):
        return pltpu.make_async_remote_copy(
            src_ref=src, dst_ref=dst, send_sem=ssem, recv_sem=rsem,
            device_id=device, device_id_type=MESH,
        )

    def obs_copy(i):
        return remote(obs_send.at[i], obs_recv.at[i], obs_ssem.at[i], obs_rsem.at[i], (me, beside[i]))

    half = groups // 2

    def mrg_copy(i, far):
        span = pl.ds((me // half ^ far) * half, half)
        return remote(
            mrg_send.at[i, span], mrg_recv.at[i, span], mrg_ssem.at[i, far], mrg_rsem.at[i, far], (me, beside[i])
        )

    def in_copy(i, peer, source):
        return remote(work.at[i, peer], cols.at[i, source], in_ssem.at[i], in_rsem.at[i], (peer, tile))

    def in_all(i):
        span = pl.ds(0, groups - 1)
        return remote(work.at[i, span], cols.at[i, span], in_ssem.at[i], in_rsem.at[i], (me ^ 1, tile))

    def out_copy(i, step):
        return remote(
            ret.at[i, me ^ step], home.at[i, step], out_ssem.at[i], out_rsem.at[i, step // half], (me ^ step, tile)
        )

    def out_part(i, part):
        span = pl.ds(0, half - 1 + part)
        return remote(ret.at[i, span], home.at[i, span], out_ssem.at[i], out_rsem.at[i, part], (me ^ 1, tile))

    def out_all(i):
        span = pl.ds(0, groups - 1)
        return remote(ret.at[i, span], home.at[i, span], out_ssem.at[i], out_rsem.at[i, 0], (me ^ 1, tile))

    def fwd_copy(i, part):
        span = pl.ds(part * half, half)
        return remote(
            home.at[i, span], back.at[i, span], fwd_ssem.at[i, part], fwd_rsem.at[i, part], (me, beside[i])
        )

    order = [*range(1, groups)]

    for far in (1, 0):
        for i in (1, 0):

            @pl.when(there[i])
            def _(i=i, far=far):
                mrg_copy(i, far).start()

    for i in (1, 0):

        @pl.when(there[i])
        def _(i=i):
            obs_copy(i).start()

    def spread_out(i):
        for far in (1, 0):
            @pl.when(there[i])
            def _(far=far):
                mrg_copy(i, far).wait_recv()

            span = pl.ds((me // half ^ far) * half, half)
            work[i, span] = jnp.where(
                takes[i], mrg_recv[i, span].astype(F32), work[i, span].astype(F32)
            ).astype(BF16)

            @pl.when(me >= 0)
            def _(far=far):
                for step in order:
                    if step // half == far:
                        in_copy(i, me ^ step, me).start()
                if not far:
                    cols[i, me] = work[i, me]

    base = members - 1.0
    eye = jnp.where(eye_obs, 1.0, 0.0)
    eye_all = lax.broadcasted_iota(jnp.int32, (members, members), 0) == lax.broadcasted_iota(
        jnp.int32, (members, members), 1
    )

    def observations(i):
        ours = observe(own[i])

        @pl.when(there[i])
        def _():
            obs_copy(i).wait_recv()

        took = jnp.where(takes[i], obs_recv[i, :obs_rows, :].astype(F32), ours[0])
        scaled = took.astype(BF16)
        took = jnp.where(takes[i], obs_recv[i, obs_rows:, :obs_rows].astype(F32), ours[1])
        return scaled, took.astype(BF16)

    def transforms(found):
        scaled, signal = zip(*[observations(i) for i in both])
        n = both
        gram = [dot(scaled[w], scaled[w], 1, 1) for w in n]
        norm, x, xc, pc, q, p = [], [], [], [], [], []
        for w in n:
            total = jnp.sum(
                gram[w] * gram[w] + (2.0 * base) * jnp.where(eye_obs, gram[w], 0.0), keepdims=True
            )
            norm.append(jnp.sqrt(total + base * base * members))
            x.append(gram[w] / norm[w])
            xc.append(base / norm[w])
            pc.append(1.5 - 0.5 * xc[w])
            q.append(-0.5 * eye)
            p.append(pc[w] * eye - 0.5 * x[w])
        for repeat in range(ITERS - 1):
            n_pass = PASSES[repeat]
            square = [mm(p[w], p[w], n_pass) for w in n]
            mixed = [
                mm(
                    jnp.concatenate(
                        [square[w], square[w] + pc[w] * p[w] + (pc[w] * pc[w]) * eye], axis=1
                    ),
                    jnp.concatenate([p[w], xc[w] * q[w]], axis=0),
                    n_pass,
                )
                for w in n
            ]
            for w in n:
                q[w] = 1.5 * q[w] - 0.5 * mixed[w]
                pc[w] = pc[w] * (1.5 - 0.5 * xc[w] * pc[w] * pc[w])
            if repeat + 2 < ITERS:
                p = [pc[w] * eye + mm(x[w], q[w], n_pass) for w in n]
            yield

        y = [signal[w].astype(F32) for w in n]
        for _ in range(2):
            y = [pc[w] * y[w] + mm(mm(y[w], q[w], 3), x[w], 3) for w in n]
        shift = [mm_exact(y[w], scaled[w])[:1] / norm[w] for w in n]
        for w in n:
            half = mm_exact(q[w] / norm[w], scaled[w])
            hh, hl = split(half)
            inverse = dot(scaled[w], hh, 0, 0) + dot(scaled[w], hl, 0, 0)
            inverse = inverse + jnp.where(eye_all, pc[w], 0.0)
            found.append((jnp.sqrt(base / norm[w]) * inverse + shift[w]).astype(BF16))
        yield

    def analyse(i, transform):
        in_all(i).wait_recv()
        states = jnp.concatenate([packing.take(cols, i, part) for part in range(parts)], axis=1)
        states = states.reshape(members, length)
        average = jnp.sum(states, axis=0, keepdims=True) * (1.0 / members)
        spread = (states - average).astype(BF16)
        result = (average + dot(transform, spread)).reshape(groups, rows, length)
        for part in range(parts):
            packing.put(ret, i, part, result[:, part * chunk:(part + 1) * chunk])

        @pl.when(me >= 0)
        def _():
            for step in order:
                out_copy(i, step).start()
            home[i, 0] = ret[i, me]

    spread_out(1)
    spread_out(0)
    transform = []
    for _ in transforms(transform):
        pass
    analyse(1, transform[1])
    analyse(0, transform[0])
    for i in both:

        @pl.when(there[i])
        def _(i=i):
            obs_copy(i).wait_send()
            for far in (1, 0):
                mrg_copy(i, far).wait_send()

        in_all(i).wait_send()

    back_row = lax.broadcasted_iota(jnp.int32, (chunk * width, 1), 0)
    position = back_row & (capacity - 1)
    live = position < here
    to_left = position < jnp.maximum(-lead, 0)
    to_right = position >= WORK - lead
    line = ((((back_row >> lcap) & (groups - 1)) ^ me) << lc) + (back_row >> lw)
    home_row = lax.broadcasted_iota(jnp.int32, (chunk * width, 2 * block), 1)
    is_first = jnp.full((chunk * width, 1), core, jnp.int32) == 0

    def forward(i):
        for part in range(2):
            out_part(i, part).wait_recv()

            @pl.when(there[i])
            def _(part=part):
                fwd_copy(i, part).start()

    def place(i):
        left_side = is_first if i == 1 else jnp.logical_not(is_first)
        over = jnp.logical_or(
            jnp.logical_and(left_side, to_left),
            jnp.logical_and(jnp.logical_not(left_side), to_right),
        )
        kept_here = jnp.logical_not(jnp.logical_or(to_left, to_right))
        ours = jnp.logical_and(kept_here, position + lead == slots[i])
        mine = jnp.logical_and(live, jnp.logical_or(ours, over))
        target = jnp.where(mine, line + jnp.where(over, block, 0), -1)
        scatter = jnp.where(home_row == target, 1.0, 0.0).astype(BF16)

        @pl.when(there[i])
        def _():
            for part in range(2):
                fwd_copy(i, part).wait_recv()

        for part in range(parts):
            span = pl.ds(part * chunk, chunk)
            found = jnp.concatenate(
                [packing.take(ref, i, part).reshape(block, length).astype(BF16) for ref in (home, back)], axis=0
            )
            placed = dot(scatter, found)
            kept = (ens_ref if i else out_ref)[span].reshape(chunk * width, length).astype(F32)
            placed = jnp.where(mine, placed, kept)
            out_ref[span] = placed.astype(BF16).reshape(chunk, width, length)

    forward(1)
    forward(0)
    place(1)
    place(0)
    for i in both:
        out_all(i).wait_send()

        @pl.when(there[i])
        def _(i=i):
            for part in range(2):
                fwd_copy(i, part).wait_send()


def on_device(ensemble, departures, innovations, precision, obs_count, tile_counts):
    groups = lax.axis_size("member")
    tiles = lax.axis_size("tile")
    rows, width, length = ensemble.shape
    capacity, obs_rows, members = departures.shape
    vmem = pl.BlockSpec(memory_space=pltpu.VMEM)
    smem = pl.BlockSpec(memory_space=pltpu.SMEM)
    hbm = pl.BlockSpec(memory_space=pl.ANY)
    dma = pltpu.SemaphoreType.DMA
    blocks = pltpu.VMEM((WORK, groups, Packing(rows, length).depth, LANES), BF16)
    seen = pltpu.VMEM((WORK, obs_rows + 16, members), BF16)
    return pl.pallas_call(
        functools.partial(kernel, tiles, groups),
        out_shape=pltpu.VMEM(ensemble.shape, BF16),
        in_specs=[smem, smem, hbm, hbm, hbm, hbm],
        out_specs=vmem,
        scratch_shapes=[
            pltpu.VMEM(ensemble.shape, BF16),
            pltpu.VMEM(departures.shape, BF16),
            pltpu.VMEM(innovations.shape, F32),
            pltpu.VMEM(precision.shape, F32),
            dma((4,)),
            blocks, blocks, blocks, seen, seen, blocks, blocks, blocks, blocks,
            dma((WORK, 2)), dma((WORK, 2)), dma((WORK,)), dma((WORK,)),
            dma((WORK,)), dma((WORK,)), dma((WORK,)), dma((WORK, 2)), dma((WORK, 2)), dma((WORK, 2)),
        ],
        compiler_params=pltpu.CompilerParams(
            collective_id=0, has_side_effects=True, vmem_limit_bytes=56 * 1024 * 1024
        ),
    )(tile_counts, obs_count, ensemble, departures, innovations, precision)


def solution(mesh):
    placed = (
        P("member", "tile", None),
        P(("tile", "member"), None, None),
        P(("tile", "member"), None),
        P(("tile", "member"), None),
        P(("tile", "member")),
        P(),
    )
    return jax.shard_map(
        on_device, mesh=mesh, in_specs=placed, out_specs=P("member", "tile", None), check_vma=False
    )
```

```python
import functools

import jax
import jax.numpy as jnp
from jax import lax
from jax.experimental import pallas as pl
from jax.experimental.pallas import tpu as pltpu
from jax.sharding import PartitionSpec as P

WORK = 2
ITERS = 6
LANES = 128
PASSES = (1, 1, 1, 3, 3)
MESH = pl.DeviceIdType.MESH
F32 = jnp.float32
BF16 = jnp.bfloat16


def dot(a, b, ca=1, cb=0):
    return lax.dot_general(a, b, (((ca,), (cb,)), ((), ())), preferred_element_type=F32)


def split(x):
    high = x.astype(BF16)
    return high, (x - high.astype(F32)).astype(BF16)


def mm(a, b, passes):
    if passes == 1:
        return dot(a.astype(BF16), b.astype(BF16))
    ah, al = split(a)
    bh, bl = split(b)
    return dot(ah, bh) + (dot(ah, bl) + dot(al, bh))


def mm_exact(a, b):
    ah, al = split(a)
    return dot(ah, b) + dot(al, b)


def log2(n):
    return n.bit_length() - 1


class Packing:
    def __init__(self, rows, length):
        self.rows, self.length = rows, length
        self.chunk = min(16, rows)
        self.parts = rows // self.chunk
        self.full, self.rest = divmod(length, LANES)
        self.per = LANES // self.rest if self.rest else 1
        self.tails = -(-self.parts // self.per) if self.rest else 0
        self.depth = self.full * rows + self.tails * self.chunk

    def places(self, part):
        found = [
            (pl.ds(f * self.rows + part * self.chunk, self.chunk), slice(0, LANES), slice(f * LANES, (f + 1) * LANES))
            for f in range(self.full)
        ]
        if self.rest:
            down, across = divmod(part, self.per)
            found.append((
                pl.ds(self.full * self.rows + down * self.chunk, self.chunk),
                slice(across * self.rest, (across + 1) * self.rest),
                slice(self.full * LANES, self.length),
            ))
        return found

    def put(self, ref, which, part, piece):
        if part == 0 and self.rest and self.parts % self.per:
            tail = pl.ds(self.full * self.rows, self.tails * self.chunk)
            ref[which, :, tail, :] = jnp.zeros((ref.shape[1], self.tails * self.chunk, LANES), BF16)
        for down, across, of in self.places(part):
            ref[which, :, down, across] = piece[:, :, of].astype(BF16)

    def rows_of(self, ref, which, part):
        wide = F32 if self.chunk % 16 else BF16
        found = [
            ref[which, :, down, across].astype(wide if across == slice(0, LANES) else F32)
            for down, across, _ in self.places(part)
        ]
        return jnp.concatenate([x.reshape(-1, x.shape[2]).astype(BF16) for x in found], axis=1)

    def take(self, ref, which, part):
        return jnp.concatenate(
            [ref[which, :, down, across].astype(F32) for down, across, _ in self.places(part)], axis=2
        )


def kernel(
    tiles, groups, counts_ref, obs_ref, ens_hbm, dep_hbm, inn_hbm, prec_hbm, out_ref,
    ens_ref, dep_ref, inn_ref, prec_ref, load_sem,
    work, mrg_send, mrg_recv, obs_send, obs_recv, cols, ret, home, back,
    mrg_ssem, mrg_rsem, obs_ssem, obs_rsem, in_ssem, in_rsem, out_ssem, out_rsem, fwd_ssem, fwd_rsem,
):
    me = lax.axis_index("member")
    tile = lax.axis_index("tile")
    rows, width, length = ens_ref.shape
    capacity, obs_rows, members = dep_ref.shape
    packing = Packing(rows, length)
    both = range(WORK)

    core = lax.rem(tile, 2)
    first = core == 0
    beside = (tile + 1 - 2 * core, tile - 1 + 2 * core)
    has_next = jnp.logical_and(beside[1] >= 0, beside[1] < tiles)
    there = (tile >= 0, has_next)

    barrier = pltpu.get_barrier_semaphore()
    for step in range(groups - 1, 0, -1):
        pl.semaphore_signal(barrier, inc=1, device_id=(me ^ step, tile), device_id_type=MESH)
    pl.semaphore_signal(barrier, inc=1, device_id=(me, beside[0]), device_id_type=MESH)

    @pl.when(has_next)
    def _():
        pl.semaphore_signal(barrier, inc=1, device_id=(me, beside[1]), device_id_type=MESH)

    loads = [
        pltpu.make_async_copy(source, kept, load_sem.at[i])
        for i, (source, kept) in enumerate(
            ((inn_hbm, inn_ref), (prec_hbm, prec_ref), (dep_hbm, dep_ref), (ens_hbm, ens_ref))
        )
    ]
    for load in loads:
        load.start()
    before = 0
    here = 0
    for other in range(tiles):
        count = counts_ref[other]
        before = before + jnp.where(other < tile, count, 0)
        here = here + jnp.where(other == tile, count, 0)
    before = before // groups
    here = here // groups
    lead = before - tile * WORK
    trail = before + here - (tile + 1) * WORK
    top = capacity - 1
    slots = (1 - core, core)
    own = [jnp.clip(slots[i] - lead, 0, top) for i in both]
    send_right = jnp.clip(WORK - lead, 0, top)
    sent = (jnp.where(first, send_right, 0), jnp.where(first, 0, send_right))
    takes = (
        jnp.where(first, trail < 0, lead > 0),
        jnp.where(first, lead > 0, trail < 0),
    )

    eye_obs = lax.broadcasted_iota(jnp.int32, (obs_rows, obs_rows), 0) == lax.broadcasted_iota(
        jnp.int32, (obs_rows, obs_rows), 1
    )
    row_ids = lax.broadcasted_iota(jnp.int32, (1, obs_rows), 1)

    def observe(index):
        weight = jnp.where(row_ids < obs_ref[index], jnp.sqrt(prec_ref[pl.ds(index, 1), :]), 0.0)
        signal = weight * inn_ref[pl.ds(index, 1), :]
        weight_col = jnp.sum(jnp.where(eye_obs, weight, 0.0), axis=1, keepdims=True)
        scaled = dep_ref[index].astype(F32) * weight_col
        return scaled, jnp.broadcast_to(signal, (16, obs_rows))

    for load in loads[:3]:
        load.wait()
    for i in both:
        scaled, signal = observe(sent[i])
        obs_send[i, :obs_rows, :] = scaled.astype(BF16)
        obs_send[i, obs_rows:, :] = jnp.zeros((16, members), BF16)
        obs_send[i, obs_rows:, :obs_rows] = signal.astype(BF16)

    chunk, parts = packing.chunk, packing.parts
    lc, lg, lw, lcap = log2(chunk), log2(groups), log2(width), log2(capacity)
    block = groups * chunk
    out_row = lax.broadcasted_iota(jnp.int32, (2 * WORK * block, 1), 0)
    slot = out_row >> (lc + lg)
    column = jnp.where(
        slot == 0, own[0], jnp.where(slot == 1, own[1], jnp.where(slot == 2, sent[0], sent[1]))
    )
    wanted = (
        ((out_row & (chunk - 1)) << lw) + (((out_row >> lc) & (groups - 1)) << lcap) + column
    )
    in_row = lax.broadcasted_iota(jnp.int32, (2 * WORK * block, chunk * width), 1)
    gather = jnp.where(in_row == wanted, 1.0, 0.0).astype(BF16)
    loads[3].wait()
    for part in range(parts):
        states = ens_ref[pl.ds(part * chunk, chunk)].reshape(chunk * width, length)
        picked = dot(gather, states)
        for s in range(2 * WORK):
            piece = picked[s * block:(s + 1) * block].reshape(groups, chunk, length)
            packing.put(work if s < WORK else mrg_send, s % WORK, part, piece)

    @pl.when(jnp.logical_not(has_next))
    def _():
        mrg_recv[1] = jnp.zeros(mrg_recv.shape[1:], BF16)
        obs_recv[1] = jnp.zeros(obs_recv.shape[1:], BF16)
        back[1] = jnp.zeros(back.shape[1:], BF16)

    pl.semaphore_wait(barrier, groups + jnp.where(has_next, 1, 0))

    def remote(src, dst, ssem, rsem, device):
        return pltpu.make_async_remote_copy(
            src_ref=src, dst_ref=dst, send_sem=ssem, recv_sem=rsem,
            device_id=device, device_id_type=MESH,
        )

    def obs_copy(i):
        return remote(obs_send.at[i], obs_recv.at[i], obs_ssem.at[i], obs_rsem.at[i], (me, beside[i]))

    half = groups // 2

    def mrg_copy(i, far):
        span = pl.ds((me // half ^ far) * half, half)
        return remote(
            mrg_send.at[i, span], mrg_recv.at[i, span], mrg_ssem.at[i, far], mrg_rsem.at[i, far], (me, beside[i])
        )

    def in_copy(i, peer, source):
        return remote(work.at[i, peer], cols.at[i, source], in_ssem.at[i], in_rsem.at[i], (peer, tile))

    def in_all(i):
        span = pl.ds(0, groups - 1)
        return remote(work.at[i, span], cols.at[i, span], in_ssem.at[i], in_rsem.at[i], (me ^ 1, tile))

    def out_copy(i, step):
        return remote(
            ret.at[i, me ^ step], home.at[i, step], out_ssem.at[i], out_rsem.at[i, step // half], (me ^ step, tile)
        )

    def out_part(i, part):
        span = pl.ds(0, half - 1 + part)
        return remote(ret.at[i, span], home.at[i, span], out_ssem.at[i], out_rsem.at[i, part], (me ^ 1, tile))

    def out_all(i):
        span = pl.ds(0, groups - 1)
        return remote(ret.at[i, span], home.at[i, span], out_ssem.at[i], out_rsem.at[i, 0], (me ^ 1, tile))

    def fwd_copy(i, part):
        span = pl.ds(part * half, half)
        return remote(
            home.at[i, span], back.at[i, span], fwd_ssem.at[i, part], fwd_rsem.at[i, part], (me, beside[i])
        )

    order = [*range(1, groups)]

    for far in (1, 0):
        for i in (1, 0):

            @pl.when(there[i])
            def _(i=i, far=far):
                mrg_copy(i, far).start()

    for i in (1, 0):

        @pl.when(there[i])
        def _(i=i):
            obs_copy(i).start()

    def spread_out(i):
        for far in (1, 0):
            @pl.when(there[i])
            def _(far=far):
                mrg_copy(i, far).wait_recv()

            span = pl.ds((me // half ^ far) * half, half)
            work[i, span] = jnp.where(
                takes[i], mrg_recv[i, span].astype(F32), work[i, span].astype(F32)
            ).astype(BF16)

            @pl.when(me >= 0)
            def _(far=far):
                for step in order:
                    if step // half == far:
                        in_copy(i, me ^ step, me).start()
                if not far:
                    cols[i, me] = work[i, me]

    base = members - 1.0
    eye = jnp.where(eye_obs, 1.0, 0.0)
    eye_all = lax.broadcasted_iota(jnp.int32, (members, members), 0) == lax.broadcasted_iota(
        jnp.int32, (members, members), 1
    )

    def observations(i):
        ours = observe(own[i])

        @pl.when(there[i])
        def _():
            obs_copy(i).wait_recv()

        took = jnp.where(takes[i], obs_recv[i, :obs_rows, :].astype(F32), ours[0])
        scaled = took.astype(BF16)
        took = jnp.where(takes[i], obs_recv[i, obs_rows:, :obs_rows].astype(F32), ours[1])
        return scaled, took.astype(BF16)

    def transforms(found):
        scaled, signal = zip(*[observations(i) for i in both])
        n = both
        gram = [dot(scaled[w], scaled[w], 1, 1) for w in n]
        norm, x, xc, pc, q, p = [], [], [], [], [], []
        for w in n:
            total = jnp.sum(
                gram[w] * gram[w] + (2.0 * base) * jnp.where(eye_obs, gram[w], 0.0), keepdims=True
            )
            norm.append(jnp.sqrt(total + base * base * members))
            x.append(gram[w] / norm[w])
            xc.append(base / norm[w])
            pc.append(1.5 - 0.5 * xc[w])
            q.append(-0.5 * eye)
            p.append(pc[w] * eye - 0.5 * x[w])
        for repeat in range(ITERS - 1):
            n_pass = PASSES[repeat]
            square = [mm(p[w], p[w], n_pass) for w in n]
            mixed = [
                mm(
                    jnp.concatenate(
                        [square[w], square[w] + pc[w] * p[w] + (pc[w] * pc[w]) * eye], axis=1
                    ),
                    jnp.concatenate([p[w], xc[w] * q[w]], axis=0),
                    n_pass,
                )
                for w in n
            ]
            for w in n:
                q[w] = 1.5 * q[w] - 0.5 * mixed[w]
                pc[w] = pc[w] * (1.5 - 0.5 * xc[w] * pc[w] * pc[w])
            if repeat + 2 < ITERS:
                p = [pc[w] * eye + mm(x[w], q[w], n_pass) for w in n]
            yield

        y = [signal[w].astype(F32) for w in n]
        for _ in range(2):
            y = [pc[w] * y[w] + mm(mm(y[w], q[w], 3), x[w], 3) for w in n]
        shift = [mm_exact(y[w], scaled[w])[:1] / norm[w] for w in n]
        for w in n:
            half = mm_exact(q[w] / norm[w], scaled[w])
            hh, hl = split(half)
            inverse = dot(scaled[w], hh, 0, 0) + dot(scaled[w], hl, 0, 0)
            inverse = inverse + jnp.where(eye_all, pc[w], 0.0)
            found.append((jnp.sqrt(base / norm[w]) * inverse + shift[w]).astype(BF16))
        yield

    def analyse(i, transform):
        in_all(i).wait_recv()
        states = jnp.concatenate([packing.take(cols, i, part) for part in range(parts)], axis=1)
        states = states.reshape(members, length)
        average = jnp.sum(states, axis=0, keepdims=True) * (1.0 / members)
        spread = (states - average).astype(BF16)
        result = (average + dot(transform, spread)).reshape(groups, rows, length)
        for part in range(parts):
            packing.put(ret, i, part, result[:, part * chunk:(part + 1) * chunk])

        @pl.when(me >= 0)
        def _():
            for step in order:
                out_copy(i, step).start()
            home[i, 0] = ret[i, me]

    spread_out(1)
    spread_out(0)
    transform = []
    for _ in transforms(transform):
        pass
    analyse(1, transform[1])
    analyse(0, transform[0])
    for i in both:

        @pl.when(there[i])
        def _(i=i):
            obs_copy(i).wait_send()
            for far in (1, 0):
                mrg_copy(i, far).wait_send()

        in_all(i).wait_send()

    back_row = lax.broadcasted_iota(jnp.int32, (chunk * width, 1), 0)
    position = back_row & (capacity - 1)
    live = position < here
    to_left = position < jnp.maximum(-lead, 0)
    to_right = position >= WORK - lead
    line = ((((back_row >> lcap) & (groups - 1)) ^ me) << lc) + (back_row >> lw)
    is_first = jnp.full((chunk * width, 1), core, jnp.int32) == 0
    stays = jnp.logical_not(jnp.logical_or(to_left, to_right))
    ours = [jnp.logical_and(stays, position + lead == slots[i]) for i in both]
    over = [
        jnp.where(is_first, a.astype(jnp.int32), b.astype(jnp.int32)) > 0
        for a, b in ((to_right, to_left), (to_left, to_right))
    ]

    def forward(i):
        for part in range(2):
            out_part(i, part).wait_recv()

            @pl.when(there[i])
            def _(part=part):
                fwd_copy(i, part).start()

    def forwarded(i):
        @pl.when(there[i])
        def _():
            for part in range(2):
                fwd_copy(i, part).wait_recv()

    def place(kept_ref, *sources):
        target = jnp.full((chunk * width, 1), -1, jnp.int32)
        for n, (_, _, mine) in enumerate(sources):
            target = jnp.where(jnp.logical_and(live, mine), line + n * block, target)
        home_row = lax.broadcasted_iota(jnp.int32, (chunk * width, len(sources) * block), 1)
        scatter = jnp.where(home_row == target, 1.0, 0.0).astype(BF16)
        for part in range(parts):
            span = pl.ds(part * chunk, chunk)
            found = jnp.concatenate([packing.rows_of(ref, i, part) for ref, i, _ in sources], axis=0)
            placed = dot(scatter, found)
            kept = kept_ref[span].reshape(chunk * width, length).astype(F32)
            placed = jnp.where(target >= 0, placed, kept)
            out_ref[span] = placed.astype(BF16).reshape(chunk, width, length)

    forward(1)
    forward(0)
    forwarded(1)
    forwarded(0)
    place(ens_ref, (home, 1, ours[1]), (back, 1, over[1]), (home, 0, ours[0]), (back, 0, over[0]))
    for i in both:
        out_all(i).wait_send()

        @pl.when(there[i])
        def _(i=i):
            for part in range(2):
                fwd_copy(i, part).wait_send()


def on_device(ensemble, departures, innovations, precision, obs_count, tile_counts):
    groups = lax.axis_size("member")
    tiles = lax.axis_size("tile")
    rows, width, length = ensemble.shape
    capacity, obs_rows, members = departures.shape
    vmem = pl.BlockSpec(memory_space=pltpu.VMEM)
    smem = pl.BlockSpec(memory_space=pltpu.SMEM)
    hbm = pl.BlockSpec(memory_space=pl.ANY)
    dma = pltpu.SemaphoreType.DMA
    blocks = pltpu.VMEM((WORK, groups, Packing(rows, length).depth, LANES), BF16)
    seen = pltpu.VMEM((WORK, obs_rows + 16, members), BF16)
    return pl.pallas_call(
        functools.partial(kernel, tiles, groups),
        out_shape=pltpu.VMEM(ensemble.shape, BF16),
        in_specs=[smem, smem, hbm, hbm, hbm, hbm],
        out_specs=vmem,
        scratch_shapes=[
            pltpu.VMEM(ensemble.shape, BF16),
            pltpu.VMEM(departures.shape, BF16),
            pltpu.VMEM(innovations.shape, F32),
            pltpu.VMEM(precision.shape, F32),
            dma((4,)),
            blocks, blocks, blocks, seen, seen, blocks, blocks, blocks, blocks,
            dma((WORK, 2)), dma((WORK, 2)), dma((WORK,)), dma((WORK,)),
            dma((WORK,)), dma((WORK,)), dma((WORK,)), dma((WORK, 2)), dma((WORK, 2)), dma((WORK, 2)),
        ],
        compiler_params=pltpu.CompilerParams(
            collective_id=0, has_side_effects=True, vmem_limit_bytes=56 * 1024 * 1024
        ),
    )(tile_counts, obs_count, ensemble, departures, innovations, precision)


def solution(mesh):
    placed = (
        P("member", "tile", None),
        P(("tile", "member"), None, None),
        P(("tile", "member"), None),
        P(("tile", "member"), None),
        P(("tile", "member")),
        P(),
    )
    return jax.shard_map(
        on_device, mesh=mesh, in_specs=placed, out_specs=P("member", "tile", None), check_vma=False
    )
```

```python
import functools

import jax
import jax.numpy as jnp
from jax import lax
from jax.experimental import pallas as pl
from jax.experimental.pallas import tpu as pltpu
from jax.sharding import PartitionSpec as P

WORK = 2
ITERS = 6
LANES = 128
PASSES = (1, 1, 1, 3, 3)
MESH = pl.DeviceIdType.MESH
F32 = jnp.float32
BF16 = jnp.bfloat16


def dot(a, b, ca=1, cb=0):
    return lax.dot_general(a, b, (((ca,), (cb,)), ((), ())), preferred_element_type=F32)


def split(x):
    high = x.astype(BF16)
    return high, (x - high.astype(F32)).astype(BF16)


def mm(a, b, passes):
    if passes == 1:
        return dot(a.astype(BF16), b.astype(BF16))
    ah, al = split(a)
    bh, bl = split(b)
    return dot(ah, bh) + (dot(ah, bl) + dot(al, bh))


def mm_exact(a, b):
    ah, al = split(a)
    return dot(ah, b) + dot(al, b)


def log2(n):
    return n.bit_length() - 1


class Packing:
    def __init__(self, rows, length):
        self.rows, self.length = rows, length
        self.chunk = min(16, rows)
        self.parts = rows // self.chunk
        self.full, self.rest = divmod(length, LANES)
        self.per = LANES // self.rest if self.rest else 1
        self.tails = -(-self.parts // self.per) if self.rest else 0
        self.depth = self.full * rows + self.tails * self.chunk

    def places(self, part):
        found = [
            (pl.ds(f * self.rows + part * self.chunk, self.chunk), slice(0, LANES), slice(f * LANES, (f + 1) * LANES))
            for f in range(self.full)
        ]
        if self.rest:
            down, across = divmod(part, self.per)
            found.append((
                pl.ds(self.full * self.rows + down * self.chunk, self.chunk),
                slice(across * self.rest, (across + 1) * self.rest),
                slice(self.full * LANES, self.length),
            ))
        return found

    def put(self, ref, which, part, piece):
        if part == 0 and self.rest and self.parts % self.per:
            tail = pl.ds(self.full * self.rows, self.tails * self.chunk)
            ref[which, :, tail, :] = jnp.zeros((ref.shape[1], self.tails * self.chunk, LANES), BF16)
        for down, across, of in self.places(part):
            ref[which, :, down, across] = piece[:, :, of].astype(BF16)

    def rows_of(self, ref, which, part):
        wide = F32 if self.chunk % 16 else BF16
        found = [
            ref[which, :, down, across].astype(wide if across == slice(0, LANES) else F32)
            for down, across, _ in self.places(part)
        ]
        return jnp.concatenate([x.reshape(-1, x.shape[2]).astype(BF16) for x in found], axis=1)

    def take(self, ref, which, part):
        return jnp.concatenate(
            [ref[which, :, down, across].astype(F32) for down, across, _ in self.places(part)], axis=2
        )


def kernel(
    tiles, groups, counts_ref, obs_ref, ens_hbm, dep_hbm, inn_hbm, prec_hbm, out_ref,
    ens_ref, dep_ref, inn_ref, prec_ref, load_sem,
    work, mrg_send, mrg_recv, obs_send, obs_recv, cols, ret, home, back,
    mrg_ssem, mrg_rsem, obs_ssem, obs_rsem, in_ssem, in_rsem, out_ssem, out_rsem, fwd_ssem, fwd_rsem,
):
    me = lax.axis_index("member")
    tile = lax.axis_index("tile")
    rows, width, length = ens_ref.shape
    capacity, obs_rows, members = dep_ref.shape
    packing = Packing(rows, length)
    both = range(WORK)

    core = lax.rem(tile, 2)
    first = core == 0
    beside = (tile + 1 - 2 * core, tile - 1 + 2 * core)
    has_next = jnp.logical_and(beside[1] >= 0, beside[1] < tiles)
    there = (tile >= 0, has_next)

    barrier = pltpu.get_barrier_semaphore()
    for step in range(groups - 1, 0, -1):
        pl.semaphore_signal(barrier, inc=1, device_id=(me ^ step, tile), device_id_type=MESH)
    pl.semaphore_signal(barrier, inc=1, device_id=(me, beside[0]), device_id_type=MESH)

    @pl.when(has_next)
    def _():
        pl.semaphore_signal(barrier, inc=1, device_id=(me, beside[1]), device_id_type=MESH)

    loads = [
        pltpu.make_async_copy(source, kept, load_sem.at[i])
        for i, (source, kept) in enumerate(
            ((inn_hbm, inn_ref), (prec_hbm, prec_ref), (dep_hbm, dep_ref), (ens_hbm, ens_ref))
        )
    ]
    for load in loads:
        load.start()
    before = 0
    here = 0
    for other in range(tiles):
        count = counts_ref[other]
        before = before + jnp.where(other < tile, count, 0)
        here = here + jnp.where(other == tile, count, 0)
    before = before // groups
    here = here // groups
    lead = before - tile * WORK
    trail = before + here - (tile + 1) * WORK
    top = capacity - 1
    slots = (1 - core, core)
    own = [jnp.clip(slots[i] - lead, 0, top) for i in both]
    send_right = jnp.clip(WORK - lead, 0, top)
    sent = (jnp.where(first, send_right, 0), jnp.where(first, 0, send_right))
    takes = (
        jnp.where(first, trail < 0, lead > 0),
        jnp.where(first, lead > 0, trail < 0),
    )

    eye_obs = lax.broadcasted_iota(jnp.int32, (obs_rows, obs_rows), 0) == lax.broadcasted_iota(
        jnp.int32, (obs_rows, obs_rows), 1
    )
    row_ids = lax.broadcasted_iota(jnp.int32, (1, obs_rows), 1)

    def observe(index):
        weight = jnp.where(row_ids < obs_ref[index], jnp.sqrt(prec_ref[pl.ds(index, 1), :]), 0.0)
        signal = weight * inn_ref[pl.ds(index, 1), :]
        weight_col = jnp.sum(jnp.where(eye_obs, weight, 0.0), axis=1, keepdims=True)
        scaled = dep_ref[index].astype(F32) * weight_col
        return scaled, jnp.broadcast_to(signal, (16, obs_rows))

    for load in loads[:3]:
        load.wait()
    for i in both:
        scaled, signal = observe(sent[i])
        obs_send[i, :obs_rows, :] = scaled.astype(BF16)
        obs_send[i, obs_rows:, :] = jnp.zeros((16, members), BF16)
        obs_send[i, obs_rows:, :obs_rows] = signal.astype(BF16)

    chunk, parts = packing.chunk, packing.parts
    lc, lg, lw, lcap = log2(chunk), log2(groups), log2(width), log2(capacity)
    block = groups * chunk
    out_row = lax.broadcasted_iota(jnp.int32, (2 * WORK * block, 1), 0)
    slot = out_row >> (lc + lg)
    column = jnp.where(
        slot == 0, own[0], jnp.where(slot == 1, own[1], jnp.where(slot == 2, sent[0], sent[1]))
    )
    wanted = (
        ((out_row & (chunk - 1)) << lw) + (((out_row >> lc) & (groups - 1)) << lcap) + column
    )
    in_row = lax.broadcasted_iota(jnp.int32, (2 * WORK * block, chunk * width), 1)
    gather = jnp.where(in_row == wanted, 1.0, 0.0).astype(BF16)
    loads[3].wait()
    for part in range(parts):
        states = ens_ref[pl.ds(part * chunk, chunk)].reshape(chunk * width, length)
        picked = dot(gather, states)
        for s in range(2 * WORK):
            piece = picked[s * block:(s + 1) * block].reshape(groups, chunk, length)
            packing.put(work if s < WORK else mrg_send, s % WORK, part, piece)

    @pl.when(jnp.logical_not(has_next))
    def _():
        mrg_recv[1] = jnp.zeros(mrg_recv.shape[1:], BF16)
        obs_recv[1] = jnp.zeros(obs_recv.shape[1:], BF16)
        back[1] = jnp.zeros(back.shape[1:], BF16)

    pl.semaphore_wait(barrier, groups + jnp.where(has_next, 1, 0))

    def remote(src, dst, ssem, rsem, device):
        return pltpu.make_async_remote_copy(
            src_ref=src, dst_ref=dst, send_sem=ssem, recv_sem=rsem,
            device_id=device, device_id_type=MESH,
        )

    def obs_copy(i):
        return remote(obs_send.at[i], obs_recv.at[i], obs_ssem.at[i], obs_rsem.at[i], (me, beside[i]))

    half = groups // 2

    def mrg_copy(i, far):
        span = pl.ds((me // half ^ far) * half, half)
        return remote(
            mrg_send.at[i, span], mrg_recv.at[i, span], mrg_ssem.at[i, far], mrg_rsem.at[i, far], (me, beside[i])
        )

    def in_copy(i, peer, source):
        return remote(work.at[i, peer], cols.at[i, source], in_ssem.at[i], in_rsem.at[i], (peer, tile))

    def in_all(i):
        span = pl.ds(0, groups - 1)
        return remote(work.at[i, span], cols.at[i, span], in_ssem.at[i], in_rsem.at[i], (me ^ 1, tile))

    def out_copy(i, step):
        return remote(
            ret.at[i, me ^ step], home.at[i, step], out_ssem.at[i], out_rsem.at[i, step // half], (me ^ step, tile)
        )

    def out_part(i, part):
        span = pl.ds(0, half - 1 + part)
        return remote(ret.at[i, span], home.at[i, span], out_ssem.at[i], out_rsem.at[i, part], (me ^ 1, tile))

    def out_all(i):
        span = pl.ds(0, groups - 1)
        return remote(ret.at[i, span], home.at[i, span], out_ssem.at[i], out_rsem.at[i, 0], (me ^ 1, tile))

    def fwd_copy(i, part):
        span = pl.ds(part * half, half)
        return remote(
            home.at[i, span], back.at[i, span], fwd_ssem.at[i, part], fwd_rsem.at[i, part], (me, beside[i])
        )

    order = [*range(1, half), *(step ^ 1 for step in range(half, groups))]

    for far in (1, 0):
        for i in (1, 0):

            @pl.when(there[i])
            def _(i=i, far=far):
                mrg_copy(i, far).start()

    for i in (1, 0):

        @pl.when(there[i])
        def _(i=i):
            obs_copy(i).start()

    def spread_out(i):
        for far in (1, 0):
            @pl.when(there[i])
            def _(far=far):
                mrg_copy(i, far).wait_recv()

            span = pl.ds((me // half ^ far) * half, half)
            work[i, span] = jnp.where(
                takes[i], mrg_recv[i, span].astype(F32), work[i, span].astype(F32)
            ).astype(BF16)

            @pl.when(me >= 0)
            def _(far=far):
                for step in order:
                    if step // half == far:
                        in_copy(i, me ^ step, me).start()
                if not far:
                    cols[i, me] = work[i, me]

    base = members - 1.0
    eye = jnp.where(eye_obs, 1.0, 0.0)
    eye_all = lax.broadcasted_iota(jnp.int32, (members, members), 0) == lax.broadcasted_iota(
        jnp.int32, (members, members), 1
    )

    def observations(i):
        ours = observe(own[i])

        @pl.when(there[i])
        def _():
            obs_copy(i).wait_recv()

        took = jnp.where(takes[i], obs_recv[i, :obs_rows, :].astype(F32), ours[0])
        scaled = took.astype(BF16)
        took = jnp.where(takes[i], obs_recv[i, obs_rows:, :obs_rows].astype(F32), ours[1])
        return scaled, took.astype(BF16)

    def transforms(found):
        scaled, signal = zip(*[observations(i) for i in both])
        n = both
        gram = [dot(scaled[w], scaled[w], 1, 1) for w in n]
        norm, x, xc, pc, q, p = [], [], [], [], [], []
        for w in n:
            total = jnp.sum(
                gram[w] * gram[w] + (2.0 * base) * jnp.where(eye_obs, gram[w], 0.0), keepdims=True
            )
            norm.append(jnp.sqrt(total + base * base * members))
            x.append(gram[w] / norm[w])
            xc.append(base / norm[w])
            pc.append(1.5 - 0.5 * xc[w])
            q.append(-0.5 * eye)
            p.append(pc[w] * eye - 0.5 * x[w])
        for repeat in range(ITERS - 1):
            n_pass = PASSES[repeat]
            square = [mm(p[w], p[w], n_pass) for w in n]
            mixed = [
                mm(
                    jnp.concatenate(
                        [square[w], square[w] + pc[w] * p[w] + (pc[w] * pc[w]) * eye], axis=1
                    ),
                    jnp.concatenate([p[w], xc[w] * q[w]], axis=0),
                    n_pass,
                )
                for w in n
            ]
            for w in n:
                q[w] = 1.5 * q[w] - 0.5 * mixed[w]
                pc[w] = pc[w] * (1.5 - 0.5 * xc[w] * pc[w] * pc[w])
            if repeat + 2 < ITERS:
                p = [pc[w] * eye + mm(x[w], q[w], n_pass) for w in n]
            yield

        y = [signal[w].astype(F32) for w in n]
        for _ in range(2):
            y = [pc[w] * y[w] + mm(mm(y[w], q[w], 3), x[w], 3) for w in n]
        shift = [mm_exact(y[w], scaled[w])[:1] / norm[w] for w in n]
        for w in n:
            half = mm_exact(q[w] / norm[w], scaled[w])
            hh, hl = split(half)
            inverse = dot(scaled[w], hh, 0, 0) + dot(scaled[w], hl, 0, 0)
            inverse = inverse + jnp.where(eye_all, pc[w], 0.0)
            found.append((jnp.sqrt(base / norm[w]) * inverse + shift[w]).astype(BF16))
        yield

    def analyse(i, transform):
        in_all(i).wait_recv()
        states = jnp.concatenate([packing.take(cols, i, part) for part in range(parts)], axis=1)
        states = states.reshape(members, length)
        average = jnp.sum(states, axis=0, keepdims=True) * (1.0 / members)
        spread = (states - average).astype(BF16)
        result = (average + dot(transform, spread)).reshape(groups, rows, length)
        for part in range(parts):
            packing.put(ret, i, part, result[:, part * chunk:(part + 1) * chunk])

        @pl.when(me >= 0)
        def _():
            for step in order:
                out_copy(i, step).start()
            home[i, 0] = ret[i, me]

    spread_out(1)
    spread_out(0)
    transform = []
    for _ in transforms(transform):
        pass
    analyse(1, transform[1])
    analyse(0, transform[0])
    for i in both:

        @pl.when(there[i])
        def _(i=i):
            obs_copy(i).wait_send()
            for far in (1, 0):
                mrg_copy(i, far).wait_send()

        in_all(i).wait_send()

    back_row = lax.broadcasted_iota(jnp.int32, (chunk * width, 1), 0)
    position = back_row & (capacity - 1)
    live = position < here
    to_left = position < jnp.maximum(-lead, 0)
    to_right = position >= WORK - lead
    line = ((((back_row >> lcap) & (groups - 1)) ^ me) << lc) + (back_row >> lw)
    is_first = jnp.full((chunk * width, 1), core, jnp.int32) == 0
    stays = jnp.logical_not(jnp.logical_or(to_left, to_right))
    ours = [jnp.logical_and(stays, position + lead == slots[i]) for i in both]
    over = [
        jnp.where(is_first, a.astype(jnp.int32), b.astype(jnp.int32)) > 0
        for a, b in ((to_right, to_left), (to_left, to_right))
    ]

    def forward(i):
        for part in range(2):
            out_part(i, part).wait_recv()

            @pl.when(there[i])
            def _(part=part):
                fwd_copy(i, part).start()

    def forwarded(i):
        @pl.when(there[i])
        def _():
            for part in range(2):
                fwd_copy(i, part).wait_recv()

    def place(kept_ref, *sources):
        target = jnp.full((chunk * width, 1), -1, jnp.int32)
        for n, (_, _, mine) in enumerate(sources):
            target = jnp.where(jnp.logical_and(live, mine), line + n * block, target)
        home_row = lax.broadcasted_iota(jnp.int32, (chunk * width, len(sources) * block), 1)
        scatter = jnp.where(home_row == target, 1.0, 0.0).astype(BF16)
        for part in range(parts):
            span = pl.ds(part * chunk, chunk)
            found = jnp.concatenate([packing.rows_of(ref, i, part) for ref, i, _ in sources], axis=0)
            placed = dot(scatter, found)
            kept = kept_ref[span].reshape(chunk * width, length).astype(F32)
            placed = jnp.where(target >= 0, placed, kept)
            out_ref[span] = placed.astype(BF16).reshape(chunk, width, length)

    forward(1)
    forward(0)
    forwarded(1)
    forwarded(0)
    place(ens_ref, (home, 1, ours[1]), (back, 1, over[1]), (home, 0, ours[0]), (back, 0, over[0]))
    for i in both:
        out_all(i).wait_send()

        @pl.when(there[i])
        def _(i=i):
            for part in range(2):
                fwd_copy(i, part).wait_send()


def on_device(ensemble, departures, innovations, precision, obs_count, tile_counts):
    groups = lax.axis_size("member")
    tiles = lax.axis_size("tile")
    rows, width, length = ensemble.shape
    capacity, obs_rows, members = departures.shape
    vmem = pl.BlockSpec(memory_space=pltpu.VMEM)
    smem = pl.BlockSpec(memory_space=pltpu.SMEM)
    hbm = pl.BlockSpec(memory_space=pl.ANY)
    dma = pltpu.SemaphoreType.DMA
    blocks = pltpu.VMEM((WORK, groups, Packing(rows, length).depth, LANES), BF16)
    seen = pltpu.VMEM((WORK, obs_rows + 16, members), BF16)
    return pl.pallas_call(
        functools.partial(kernel, tiles, groups),
        out_shape=pltpu.VMEM(ensemble.shape, BF16),
        in_specs=[smem, smem, hbm, hbm, hbm, hbm],
        out_specs=vmem,
        scratch_shapes=[
            pltpu.VMEM(ensemble.shape, BF16),
            pltpu.VMEM(departures.shape, BF16),
            pltpu.VMEM(innovations.shape, F32),
            pltpu.VMEM(precision.shape, F32),
            dma((4,)),
            blocks, blocks, blocks, seen, seen, blocks, blocks, blocks, blocks,
            dma((WORK, 2)), dma((WORK, 2)), dma((WORK,)), dma((WORK,)),
            dma((WORK,)), dma((WORK,)), dma((WORK,)), dma((WORK, 2)), dma((WORK, 2)), dma((WORK, 2)),
        ],
        compiler_params=pltpu.CompilerParams(
            collective_id=0, has_side_effects=True, vmem_limit_bytes=56 * 1024 * 1024
        ),
    )(tile_counts, obs_count, ensemble, departures, innovations, precision)


def solution(mesh):
    placed = (
        P("member", "tile", None),
        P(("tile", "member"), None, None),
        P(("tile", "member"), None),
        P(("tile", "member"), None),
        P(("tile", "member")),
        P(),
    )
    return jax.shard_map(
        on_device, mesh=mesh, in_specs=placed, out_specs=P("member", "tile", None), check_vma=False
    )
```

```python
import functools

import jax
import jax.numpy as jnp
from jax import lax
from jax.experimental import pallas as pl
from jax.experimental.pallas import tpu as pltpu
from jax.sharding import PartitionSpec as P

WORK = 2
ITERS = 6
LANES = 128
PASSES = (1, 1, 1, 3, 3)
MESH = pl.DeviceIdType.MESH
F32 = jnp.float32
BF16 = jnp.bfloat16


def dot(a, b, ca=1, cb=0):
    return lax.dot_general(a, b, (((ca,), (cb,)), ((), ())), preferred_element_type=F32)


def split(x):
    high = x.astype(BF16)
    return high, (x - high.astype(F32)).astype(BF16)


def mm(a, b, passes):
    if passes == 1:
        return dot(a.astype(BF16), b.astype(BF16))
    ah, al = split(a)
    bh, bl = split(b)
    return dot(ah, bh) + (dot(ah, bl) + dot(al, bh))


def mm_exact(a, b):
    ah, al = split(a)
    return dot(ah, b) + dot(al, b)


def log2(n):
    return n.bit_length() - 1


class Packing:
    def __init__(self, rows, length):
        self.rows, self.length = rows, length
        self.chunk = min(16, rows)
        self.parts = rows // self.chunk
        self.full, self.rest = divmod(length, LANES)
        self.per = LANES // self.rest if self.rest else 1
        self.tails = -(-self.parts // self.per) if self.rest else 0
        self.depth = self.full * rows + self.tails * self.chunk

    def places(self, part):
        found = [
            (pl.ds(f * self.rows + part * self.chunk, self.chunk), slice(0, LANES), slice(f * LANES, (f + 1) * LANES))
            for f in range(self.full)
        ]
        if self.rest:
            down, across = divmod(part, self.per)
            found.append((
                pl.ds(self.full * self.rows + down * self.chunk, self.chunk),
                slice(across * self.rest, (across + 1) * self.rest),
                slice(self.full * LANES, self.length),
            ))
        return found

    def put(self, ref, which, part, piece):
        if part == 0 and self.rest and self.parts % self.per:
            tail = pl.ds(self.full * self.rows, self.tails * self.chunk)
            ref[which, :, tail, :] = jnp.zeros((ref.shape[1], self.tails * self.chunk, LANES), BF16)
        for down, across, of in self.places(part):
            ref[which, :, down, across] = piece[:, :, of].astype(BF16)

    def rows_of(self, ref, which, part):
        wide = F32 if self.chunk % 16 else BF16
        found = [
            ref[which, :, down, across].astype(wide if across == slice(0, LANES) else F32)
            for down, across, _ in self.places(part)
        ]
        return jnp.concatenate([x.reshape(-1, x.shape[2]).astype(BF16) for x in found], axis=1)

    def take(self, ref, which, part):
        return jnp.concatenate(
            [ref[which, :, down, across].astype(F32) for down, across, _ in self.places(part)], axis=2
        )


def kernel(
    tiles, groups, counts_ref, obs_ref, ens_hbm, dep_hbm, inn_hbm, prec_hbm, out_ref,
    ens_ref, dep_ref, inn_ref, prec_ref, load_sem,
    work, mrg_send, mrg_recv, obs_send, obs_recv, cols, ret, home, back,
    mrg_ssem, mrg_rsem, obs_ssem, obs_rsem, in_ssem, in_rsem, out_ssem, out_rsem, fwd_ssem, fwd_rsem,
):
    me = lax.axis_index("member")
    tile = lax.axis_index("tile")
    rows, width, length = ens_ref.shape
    capacity, obs_rows, members = dep_ref.shape
    packing = Packing(rows, length)
    both = range(WORK)

    core = lax.rem(tile, 2)
    first = core == 0
    beside = (tile + 1 - 2 * core, tile - 1 + 2 * core)
    has_next = jnp.logical_and(beside[1] >= 0, beside[1] < tiles)
    there = (tile >= 0, has_next)

    barrier = pltpu.get_barrier_semaphore()
    for step in range(groups - 1, 0, -1):
        pl.semaphore_signal(barrier, inc=1, device_id=(me ^ step, tile), device_id_type=MESH)
    pl.semaphore_signal(barrier, inc=1, device_id=(me, beside[0]), device_id_type=MESH)

    @pl.when(has_next)
    def _():
        pl.semaphore_signal(barrier, inc=1, device_id=(me, beside[1]), device_id_type=MESH)

    loads = [
        pltpu.make_async_copy(source, kept, load_sem.at[i])
        for i, (source, kept) in enumerate(
            ((inn_hbm, inn_ref), (prec_hbm, prec_ref), (dep_hbm, dep_ref), (ens_hbm, ens_ref))
        )
    ]
    for load in loads:
        load.start()
    before = 0
    here = 0
    for other in range(tiles):
        count = counts_ref[other]
        before = before + jnp.where(other < tile, count, 0)
        here = here + jnp.where(other == tile, count, 0)
    before = before // groups
    here = here // groups
    lead = before - tile * WORK
    trail = before + here - (tile + 1) * WORK
    top = capacity - 1
    slots = (1 - core, core)
    own = [jnp.clip(slots[i] - lead, 0, top) for i in both]
    send_right = jnp.clip(WORK - lead, 0, top)
    sent = (jnp.where(first, send_right, 0), jnp.where(first, 0, send_right))
    takes = (
        jnp.where(first, trail < 0, lead > 0),
        jnp.where(first, lead > 0, trail < 0),
    )

    eye_obs = lax.broadcasted_iota(jnp.int32, (obs_rows, obs_rows), 0) == lax.broadcasted_iota(
        jnp.int32, (obs_rows, obs_rows), 1
    )
    row_ids = lax.broadcasted_iota(jnp.int32, (1, obs_rows), 1)

    def observe(index):
        weight = jnp.where(row_ids < obs_ref[index], jnp.sqrt(prec_ref[pl.ds(index, 1), :]), 0.0)
        signal = weight * inn_ref[pl.ds(index, 1), :]
        weight_col = jnp.sum(jnp.where(eye_obs, weight, 0.0), axis=1, keepdims=True)
        scaled = dep_ref[index].astype(F32) * weight_col
        return scaled, jnp.broadcast_to(signal, (16, obs_rows))

    for load in loads[:3]:
        load.wait()
    for i in both:
        scaled, signal = observe(sent[i])
        obs_send[i, :obs_rows, :] = scaled.astype(BF16)
        obs_send[i, obs_rows:, :] = jnp.zeros((16, members), BF16)
        obs_send[i, obs_rows:, :obs_rows] = signal.astype(BF16)

    chunk, parts = packing.chunk, packing.parts
    lc, lg, lw, lcap = log2(chunk), log2(groups), log2(width), log2(capacity)
    block = groups * chunk
    out_row = lax.broadcasted_iota(jnp.int32, (2 * WORK * block, 1), 0)
    slot = out_row >> (lc + lg)
    column = jnp.where(
        slot == 0, own[0], jnp.where(slot == 1, own[1], jnp.where(slot == 2, sent[0], sent[1]))
    )
    wanted = (
        ((out_row & (chunk - 1)) << lw) + (((out_row >> lc) & (groups - 1)) << lcap) + column
    )
    in_row = lax.broadcasted_iota(jnp.int32, (2 * WORK * block, chunk * width), 1)
    gather = jnp.where(in_row == wanted, 1.0, 0.0).astype(BF16)
    loads[3].wait()
    for part in range(parts):
        states = ens_ref[pl.ds(part * chunk, chunk)].reshape(chunk * width, length)
        picked = dot(gather, states)
        for s in range(2 * WORK):
            piece = picked[s * block:(s + 1) * block].reshape(groups, chunk, length)
            packing.put(work if s < WORK else mrg_send, s % WORK, part, piece)

    @pl.when(jnp.logical_not(has_next))
    def _():
        mrg_recv[1] = jnp.zeros(mrg_recv.shape[1:], BF16)
        obs_recv[1] = jnp.zeros(obs_recv.shape[1:], BF16)
        back[1] = jnp.zeros(back.shape[1:], BF16)

    pl.semaphore_wait(barrier, groups + jnp.where(has_next, 1, 0))

    def remote(src, dst, ssem, rsem, device):
        return pltpu.make_async_remote_copy(
            src_ref=src, dst_ref=dst, send_sem=ssem, recv_sem=rsem,
            device_id=device, device_id_type=MESH,
        )

    def obs_copy(i):
        return remote(obs_send.at[i], obs_recv.at[i], obs_ssem.at[i], obs_rsem.at[i], (me, beside[i]))

    half = groups // 2

    def mrg_copy(i, far):
        span = pl.ds((me // half ^ far) * half, half)
        return remote(
            mrg_send.at[i, span], mrg_recv.at[i, span], mrg_ssem.at[i, far], mrg_rsem.at[i, far], (me, beside[i])
        )

    def in_copy(i, peer, source):
        return remote(work.at[i, peer], cols.at[i, source], in_ssem.at[i], in_rsem.at[i], (peer, tile))

    def in_all(i):
        span = pl.ds(0, groups - 1)
        return remote(work.at[i, span], cols.at[i, span], in_ssem.at[i], in_rsem.at[i], (me ^ 1, tile))

    def out_copy(i, step):
        return remote(
            ret.at[i, me ^ step], home.at[i, step], out_ssem.at[i], out_rsem.at[i, step // half], (me ^ step, tile)
        )

    def out_part(i, part):
        span = pl.ds(0, half - 1 + part)
        return remote(ret.at[i, span], home.at[i, span], out_ssem.at[i], out_rsem.at[i, part], (me ^ 1, tile))

    def out_all(i):
        span = pl.ds(0, groups - 1)
        return remote(ret.at[i, span], home.at[i, span], out_ssem.at[i], out_rsem.at[i, 0], (me ^ 1, tile))

    def fwd_copy(i, part):
        span = pl.ds(part * half, half)
        return remote(
            home.at[i, span], back.at[i, span], fwd_ssem.at[i, part], fwd_rsem.at[i, part], (me, beside[i])
        )

    order = [1, *(step ^ 1 for step in range(2, groups))]

    for far in (1, 0):
        for i in (1, 0):

            @pl.when(there[i])
            def _(i=i, far=far):
                mrg_copy(i, far).start()

    for i in (1, 0):

        @pl.when(there[i])
        def _(i=i):
            obs_copy(i).start()

    def spread_out(i):
        for far in (1, 0):
            @pl.when(there[i])
            def _(far=far):
                mrg_copy(i, far).wait_recv()

            span = pl.ds((me // half ^ far) * half, half)
            work[i, span] = jnp.where(takes[i], mrg_recv[i, span], work[i, span])

            @pl.when(me >= 0)
            def _(far=far):
                for step in order:
                    if step // half == far:
                        in_copy(i, me ^ step, me).start()
                if not far:
                    cols[i, me] = work[i, me]

    base = members - 1.0
    eye = jnp.where(eye_obs, 1.0, 0.0)
    eye_all = lax.broadcasted_iota(jnp.int32, (members, members), 0) == lax.broadcasted_iota(
        jnp.int32, (members, members), 1
    )

    def observations(i):
        ours = observe(own[i])

        @pl.when(there[i])
        def _():
            obs_copy(i).wait_recv()

        took = jnp.where(takes[i], obs_recv[i, :obs_rows, :].astype(F32), ours[0])
        scaled = took.astype(BF16)
        took = jnp.where(takes[i], obs_recv[i, obs_rows:, :obs_rows].astype(F32), ours[1])
        return scaled, took.astype(BF16)

    def transforms(found):
        scaled, signal = zip(*[observations(i) for i in both])
        n = both
        gram = [dot(scaled[w], scaled[w], 1, 1) for w in n]
        norm, x, xc, pc, q, p = [], [], [], [], [], []
        for w in n:
            total = jnp.sum(
                gram[w] * gram[w] + (2.0 * base) * jnp.where(eye_obs, gram[w], 0.0), keepdims=True
            )
            norm.append(jnp.sqrt(total + base * base * members))
            x.append(gram[w] / norm[w])
            xc.append(base / norm[w])
            pc.append(1.5 - 0.5 * xc[w])
            q.append(-0.5 * eye)
            p.append(pc[w] * eye - 0.5 * x[w])
        for repeat in range(ITERS - 1):
            n_pass = PASSES[repeat]
            square = [mm(p[w], p[w], n_pass) for w in n]
            mixed = [
                mm(
                    jnp.concatenate(
                        [square[w], square[w] + pc[w] * p[w] + (pc[w] * pc[w]) * eye], axis=1
                    ),
                    jnp.concatenate([p[w], xc[w] * q[w]], axis=0),
                    n_pass,
                )
                for w in n
            ]
            for w in n:
                q[w] = 1.5 * q[w] - 0.5 * mixed[w]
                pc[w] = pc[w] * (1.5 - 0.5 * xc[w] * pc[w] * pc[w])
            if repeat + 2 < ITERS:
                p = [pc[w] * eye + mm(x[w], q[w], n_pass) for w in n]
            yield

        y = [signal[w].astype(F32) for w in n]
        for _ in range(2):
            y = [pc[w] * y[w] + mm(mm(y[w], q[w], 3), x[w], 3) for w in n]
        shift = [mm_exact(y[w], scaled[w])[:1] / norm[w] for w in n]
        for w in n:
            half = mm_exact(q[w] / norm[w], scaled[w])
            hh, hl = split(half)
            inverse = dot(scaled[w], hh, 0, 0) + dot(scaled[w], hl, 0, 0)
            inverse = inverse + jnp.where(eye_all, pc[w], 0.0)
            found.append((jnp.sqrt(base / norm[w]) * inverse + shift[w]).astype(BF16))
        yield

    def analyse(i, transform):
        in_all(i).wait_recv()
        states = jnp.concatenate([packing.take(cols, i, part) for part in range(parts)], axis=1)
        states = states.reshape(members, length)
        average = jnp.sum(states, axis=0, keepdims=True) * (1.0 / members)
        spread = (states - average).astype(BF16)
        result = (average + dot(transform, spread)).reshape(groups, rows, length)
        for part in range(parts):
            packing.put(ret, i, part, result[:, part * chunk:(part + 1) * chunk])

        @pl.when(me >= 0)
        def _():
            for step in order:
                out_copy(i, step).start()
            home[i, 0] = ret[i, me]

    spread_out(1)
    spread_out(0)
    transform = []
    for _ in transforms(transform):
        pass
    analyse(1, transform[1])
    analyse(0, transform[0])
    for i in both:

        @pl.when(there[i])
        def _(i=i):
            obs_copy(i).wait_send()
            for far in (1, 0):
                mrg_copy(i, far).wait_send()

        in_all(i).wait_send()

    back_row = lax.broadcasted_iota(jnp.int32, (chunk * width, 1), 0)
    position = back_row & (capacity - 1)
    live = position < here
    to_left = position < jnp.maximum(-lead, 0)
    to_right = position >= WORK - lead
    line = ((((back_row >> lcap) & (groups - 1)) ^ me) << lc) + (back_row >> lw)
    is_first = jnp.full((chunk * width, 1), core, jnp.int32) == 0
    stays = jnp.logical_not(jnp.logical_or(to_left, to_right))
    ours = [jnp.logical_and(stays, position + lead == slots[i]) for i in both]
    over = [
        jnp.where(is_first, a.astype(jnp.int32), b.astype(jnp.int32)) > 0
        for a, b in ((to_right, to_left), (to_left, to_right))
    ]

    def forward(i):
        for part in range(2):
            out_part(i, part).wait_recv()

            @pl.when(there[i])
            def _(part=part):
                fwd_copy(i, part).start()

    def forwarded(i):
        @pl.when(there[i])
        def _():
            for part in range(2):
                fwd_copy(i, part).wait_recv()

    def place(kept_ref, *sources):
        target = jnp.full((chunk * width, 1), -1, jnp.int32)
        for n, (_, _, mine) in enumerate(sources):
            target = jnp.where(jnp.logical_and(live, mine), line + n * block, target)
        home_row = lax.broadcasted_iota(jnp.int32, (chunk * width, len(sources) * block), 1)
        scatter = jnp.where(home_row == target, 1.0, 0.0).astype(BF16)
        for part in range(parts):
            span = pl.ds(part * chunk, chunk)
            found = jnp.concatenate([packing.rows_of(ref, i, part) for ref, i, _ in sources], axis=0)
            placed = dot(scatter, found)
            kept = kept_ref[span].reshape(chunk * width, length).astype(F32)
            placed = jnp.where(target >= 0, placed, kept)
            out_ref[span] = placed.astype(BF16).reshape(chunk, width, length)

    forward(1)
    forward(0)
    forwarded(1)
    for i in both:
        out_all(i).wait_send()

        @pl.when(there[i])
        def _(i=i):
            for part in range(2):
                fwd_copy(i, part).wait_send()

    forwarded(0)
    place(ens_ref, (home, 1, ours[1]), (back, 1, over[1]), (home, 0, ours[0]), (back, 0, over[0]))


def on_device(ensemble, departures, innovations, precision, obs_count, tile_counts):
    groups = lax.axis_size("member")
    tiles = lax.axis_size("tile")
    rows, width, length = ensemble.shape
    capacity, obs_rows, members = departures.shape
    vmem = pl.BlockSpec(memory_space=pltpu.VMEM)
    smem = pl.BlockSpec(memory_space=pltpu.SMEM)
    hbm = pl.BlockSpec(memory_space=pl.ANY)
    dma = pltpu.SemaphoreType.DMA
    blocks = pltpu.VMEM((WORK, groups, Packing(rows, length).depth, LANES), BF16)
    seen = pltpu.VMEM((WORK, obs_rows + 16, members), BF16)
    return pl.pallas_call(
        functools.partial(kernel, tiles, groups),
        out_shape=pltpu.VMEM(ensemble.shape, BF16),
        in_specs=[smem, smem, hbm, hbm, hbm, hbm],
        out_specs=vmem,
        scratch_shapes=[
            pltpu.VMEM(ensemble.shape, BF16),
            pltpu.VMEM(departures.shape, BF16),
            pltpu.VMEM(innovations.shape, F32),
            pltpu.VMEM(precision.shape, F32),
            dma((4,)),
            blocks, blocks, blocks, seen, seen, blocks, blocks, blocks, blocks,
            dma((WORK, 2)), dma((WORK, 2)), dma((WORK,)), dma((WORK,)),
            dma((WORK,)), dma((WORK,)), dma((WORK,)), dma((WORK, 2)), dma((WORK, 2)), dma((WORK, 2)),
        ],
        compiler_params=pltpu.CompilerParams(
            collective_id=0, has_side_effects=True, vmem_limit_bytes=56 * 1024 * 1024
        ),
    )(tile_counts, obs_count, ensemble, departures, innovations, precision)


def solution(mesh):
    placed = (
        P("member", "tile", None),
        P(("tile", "member"), None, None),
        P(("tile", "member"), None),
        P(("tile", "member"), None),
        P(("tile", "member")),
        P(),
    )
    return jax.shard_map(
        on_device, mesh=mesh, in_specs=placed, out_specs=P("member", "tile", None), check_vma=False
    )
```
